256 devices in a mesh: seq: 32 (over x, z), head: 8 (over y, core).
Axes of the slice: x: 4, y: 4, z: 8, core: 2. Of those that a mesh axis runs over, the one named last changes fastest.
Arguments:
- tokens: bfloat16 [24576, 4096], P('seq'), may hold values from -6 to 6
- qkv_weight: bfloat16 [3, 4096, 4096], P(None, 'seq', 'head'), may hold values from -0.09375 to 0.09375
- out_weight: bfloat16 [4096, 4096], P('head', 'seq'), may hold values from -0.09375 to 0.09375
- out_gain: float32 [4096], P('head'), may hold values from 0.25 to 1.75
Outputs:
- mixed: bfloat16 [24576, 4096], P('seq', 'head')
The draws below stay inside these ranges and needn't reach their ends.
All inputs are finite; a program needn't handle non-finite values.
Results may differ from the reference program's by a relative error of at most 0.019.
Values may be sent and summed in bfloat16 or wider, within the bound.
No kernel may reach another device: no remote copies, remote signals or barrier semaphores. Data moves between devices by JAX's collectives and lax.ppermute only.
A program may use at most 64 MiB of HBM per device.

```python
import jax
import jax.numpy as jnp
from jax import lax

D = 4096
HEADS = 32
HEAD_DIM = 128
TOK_DEV = 768
TOKENS = 24576
N_SEQ = 32
N_HEAD = 8


def shard_levels(key, extent, shards, least, top_value):
    def one(position, shards_of):
        draws = jax.random.uniform(jax.random.fold_in(jax.random.fold_in(key, 6), position), (shards_of,), jnp.float32, least / len(shards), top_value / len(shards))
        return jnp.repeat(jnp.exp(draws), extent[position] // shards_of).reshape((-1,) + (1,) * (len(extent) - position - 1))

    level = one(*shards[0])
    for cut in shards[1:]:
        level = level * one(*cut)
    return level


def centred(rng, shape, width, most, cuts=(), held_as=jnp.bfloat16):
    drawn = jax.random.normal(rng, shape, jnp.float32) * width
    if len(cuts) > 0:
        drawn = shard_levels(rng, shape, cuts, -0.22, 0.18) * drawn
    return jnp.clip(drawn, min=-most, max=most).astype(held_as)


def setup_inputs(seed: int = 0) -> dict:
    key_of = jax.random.split(jax.random.key(seed), 5)
    tokens = centred(key_of[0], (TOKENS, D), 1.0, 6.0, ((0, 32),))
    qkv_weight = centred(key_of[1], (3, D, D), D ** -0.5, 0.09375, ((1, 32), (2, 8)))
    out_weight = centred(key_of[2], (D, D), D ** -0.5, 0.09375, ((0, 8), (1, 32)))
    out_gain = jnp.clip(1.0 + 0.15 * jax.random.normal(key_of[3], (D,), jnp.float32), 0.25, 1.75)
    return {"tokens": tokens, "qkv_weight": qkv_weight, "out_weight": out_weight, "out_gain": out_gain}


def reference(tokens, qkv_weight, out_weight, out_gain):
    projected = jnp.stack([jnp.dot(tokens, qkv_weight[which], preferred_element_type=jnp.float32) for which in range(3)]).astype(jnp.bfloat16)
    shaped = projected.reshape(3, N_SEQ, TOK_DEV, HEADS, HEAD_DIM)
    query_matrix, keys_all, values_all = (shaped[0], shaped[1], shaped[2])

    def block_state(state_pair):
        return jnp.einsum('sbq,sbn->bqn', state_pair[0].astype(jnp.float32), state_pair[1].astype(jnp.float32))
    states = lax.map(block_state, (keys_all, values_all))
    prefix_state_sum = jnp.cumsum(states, axis=0) - states
    causal = jnp.tril(jnp.ones((TOK_DEV, TOK_DEV), dtype=bool))

    def one_block(items):
        query_block_rows, key_blk, value_blk, prefix_state_block = items
        scores = jnp.einsum('thk,shk->hts', query_block_rows.astype(jnp.float32), key_blk.astype(jnp.float32))
        scores = jnp.where(causal[None], scores, 0.0).astype(jnp.bfloat16)
        local = jnp.einsum('hts,shv->thv', scores.astype(jnp.float32), value_blk.astype(jnp.float32))
        carried_state = jnp.einsum('mal,alr->mar', query_block_rows.astype(jnp.float32), prefix_state_block.astype(jnp.bfloat16).astype(jnp.float32))
        attended = local + carried_state
        inv_scale = lax.rsqrt(lax.optimization_barrier(jnp.mean(attended * attended, axis=-1, keepdims=True)) + 1e-06)
        return ((attended * inv_scale).reshape(TOK_DEV, D) * out_gain).astype(jnp.bfloat16)
    normed = lax.map(one_block, (query_matrix, keys_all, values_all, prefix_state_sum)).reshape(TOKENS, D)
    group = D // N_HEAD
    mixed = jnp.zeros((TOKENS, D), jnp.float32)
    for index in range(N_HEAD):
        part = jnp.dot(normed[:, index * group:(index + 1) * group], out_weight[index * group:(index + 1) * group], preferred_element_type=jnp.float32)
        mixed = mixed + part.astype(jnp.bfloat16).astype(jnp.float32)
    return mixed.astype(jnp.bfloat16)
```

```python
import jax
import jax.numpy as jnp
from jax import lax
from jax.sharding import PartitionSpec as P

HEAD_DIM = 128
NX, NY, NZ = 4, 4, 8
DX = (0, -1, 1, 2)
DZ = (0, -1, 1, -2, 2, -3, 3, 4)


def seq_of(x, z):
    return (x % NX) * NZ + z % NZ


def shift(array, dx, dz):
    pairs = [(seq_of(x, z), seq_of(x + dx, z + dz)) for x in range(NX) for z in range(NZ)]
    return lax.ppermute(array, "seq", pairs)


def shift_y(array, dy):
    pairs = [(y * 2 + c, (y + dy) % NY * 2 + c) for y in range(NY) for c in range(2)]
    return lax.ppermute(array, "head", pairs)


def swap_core(array):
    return lax.ppermute(array, "head", [(h, h ^ 1) for h in range(NY * 2)])


def transpose_xy(array):
    pairs = [
        (seq_of(x, z) * 8 + y * 2 + c, seq_of(y, z) * 8 + x * 2 + c)
        for x in range(NX) for y in range(NY) for z in range(NZ) for c in range(2)
    ]
    return lax.ppermute(array, ("seq", "head"), pairs)


def after(array, *others):
    return lax.optimization_barrier((array, *others))[0]


def small_x(block):
    return [block, shift(block, 1, 0), shift(block, -1, 0), shift(block, 2, 0)]


def ring_x(block, far=0):
    half = block.shape[0] // 2
    left = shift(block, 1, 0)
    right = shift(block, -1, 0)
    if far > 0:
        opposite = shift(left, 1, 0)
    elif far < 0:
        opposite = shift(right, -1, 0)
    else:
        opposite = jnp.concatenate([shift(left[:half], 1, 0), shift(right[half:], -1, 0)])
    return [block, left, right, opposite]


def ring_z(block, far):
    blocks = [block]
    up = down = block
    for _ in range(3):
        up, down = shift(up, 0, 1), shift(down, 0, -1)
        blocks += [up, down]
    blocks.append(shift(up, 0, 1) if far > 0 else shift(down, 0, -1))
    return blocks


def ring_y(block, far):
    left = shift_y(block, 1)
    right = shift_y(block, -1)
    return [block, left, right, shift_y(left, 1) if far > 0 else shift_y(right, -1)]


def columns(tokens, blocks):
    parts = [lax.dynamic_slice_in_dim(tokens, at * HEAD_DIM, HEAD_DIM, 1) for at in blocks]
    return lax.optimization_barrier(jnp.concatenate(parts, axis=1))


def dot(a, b):
    return jnp.dot(a, b, preferred_element_type=jnp.float32)


def project(tokens, blocks):
    total = dot(tokens[0], blocks[0])
    for t, block in zip(tokens[1:], blocks[1:]):
        total = total + dot(t, block)
    return total.astype(jnp.bfloat16)


def carried(state):
    pieces = state.astype(jnp.bfloat16).reshape(NX * NZ, -1, HEAD_DIM)
    theirs = lax.all_to_all(pieces, "seq", 0, 0)
    earlier = jnp.tril(jnp.ones((NX * NZ, NX * NZ), jnp.bfloat16), -1)
    sums = jnp.einsum("ij,jrc->irc", earlier, theirs, preferred_element_type=jnp.float32)
    mine = lax.all_to_all(sums.astype(jnp.bfloat16), "seq", 0, 0)
    return mine.reshape(state.shape)


def attend(query, key, value, prefix, gain):
    rows = query.shape[0]
    causal = lax.broadcasted_iota(jnp.int32, (rows, rows), 0) >= lax.broadcasted_iota(jnp.int32, (rows, rows), 1)
    outs = []
    for h in range(query.shape[1] // HEAD_DIM):
        at = slice(h * HEAD_DIM, (h + 1) * HEAD_DIM)
        q, k, v = query[:, at], key[:, at], value[:, at]
        scores = lax.dot_general(q, k, (((1,), (1,)), ((), ())), preferred_element_type=jnp.float32)
        scores = jnp.where(causal, scores, 0.0).astype(jnp.bfloat16)
        attended = dot(scores, v) + dot(q, prefix[h])
        inv_scale = lax.rsqrt(jnp.mean(attended * attended, axis=-1, keepdims=True) + 1e-06)
        outs.append((attended * inv_scale * gain[at]).astype(jnp.bfloat16))
    return jnp.concatenate(outs, axis=1)


def per_device(tokens, qkv_weight, out_weight, out_gain):
    width = qkv_weight.shape[2]
    half = width // 2
    wq, wk, wv = qkv_weight[0], qkv_weight[1], qkv_weight[2]
    place = lax.axis_index("seq")
    x, z = place // NZ, place % NZ
    head = lax.axis_index("head")
    y, core = head // 2, head % 2
    tok_z = [columns(tokens, [(x + dx) % NX * NZ + (z + dz) % NZ for dx in DX]) for dz in DZ]
    tok_x = [columns(tokens, [(x + dx) % NX * NZ + (z + dz) % NZ for dz in DZ]) for dx in DX]

    by_x = jnp.concatenate(small_x(jnp.concatenate([wk, wq[:, :half]], axis=1)))
    by_z = jnp.concatenate(ring_z(jnp.concatenate([wv, wq[:, half:]], axis=1), -1))
    moved = transpose_xy(out_weight)
    ring_k = ring_z(jnp.concatenate([by_x[:, :width], moved], axis=1), 1)
    ring_v = ring_x(by_z[:, :width])
    key = project(tok_z, [b[:, :width] for b in ring_k])
    value = project(tok_x, ring_v)
    state = jnp.stack([
        lax.dot_general(key[:, h:h + HEAD_DIM], value[:, h:h + HEAD_DIM], (((0,), (0,)), ((), ())),
                        preferred_element_type=jnp.float32)
        for h in range(0, width, HEAD_DIM)
    ])
    prefix = carried(state)
    query_a = project(tok_z, ring_z(after(by_x[:, width:], ring_k[5]), -1))
    ring_q = ring_x(after(by_z[:, width:], ring_v[1]), -1)
    query_b = project(tok_x, ring_q)

    outs = jnp.zeros((2, width, width), out_weight.dtype)
    for dz, block in zip(DZ, ring_k):
        at = (z + dz) % NZ
        outs = lax.dynamic_update_slice(outs, block[None, :, width:], (at // 4, 0, at % 4 * HEAD_DIM))
    ring_o = ring_x(after(outs.reshape(2 * width, width), ring_q[1]), 1)
    outs = jnp.stack([ring_o[i] for i in (0, 2, 3, 1)]).reshape(NX, 2, width, width)

    normed = []
    for n, query in enumerate((query_a, query_b)):
        at = slice(n * half, (n + 1) * half)
        here = attend(query, key[:, at], value[:, at], prefix[2 * n:2 * n + 2], out_gain[at])
        normed.append(ring_y(here, 1 - 2 * n))

    def mix(part):
        total = None
        for i, dy in enumerate(DX):
            for n in range(2):
                weight = lax.dynamic_slice(outs, ((y + dy - x) % NX, part, n * half, 0), (1, 1, half, width))[0, 0]
                piece = dot(normed[n][i], weight)
                total = piece if total is None else total + piece
        return total

    theirs = swap_core(mix(1 - core).astype(jnp.bfloat16))
    return (mix(core) + theirs.astype(jnp.float32)).astype(jnp.bfloat16)


def solution(mesh):
    return jax.shard_map(
        per_device,
        mesh=mesh,
        in_specs=(P("seq", None), P(None, "seq", "head"), P("head", "seq"), P("head")),
        out_specs=P("seq", "head"),
        check_vma=False,
    )
```
